32 devices in a mesh: layer: 16 (over z, x, core), row: 2 (over y).
Axes of the slice: x: 2, y: 2, z: 4, core: 2. Of those that a mesh axis runs over, the one named last changes fastest.
Arguments:
- waves: bfloat16 [16, 3072, 512], P('layer', 'row'), may hold values from -6 to 6
- operators: bfloat16 [16, 4, 3072, 3072], P('layer', None, 'row'), may hold values from -0.0546875 to 0.0546875
- sources: bfloat16 [3072, 512], P('row'), may hold values from -6 to 6
- source_layer: int32 [128], replicated, may hold values from 0 to 15
Outputs:
- traces: bfloat16 [16, 3072, 512], P('layer', 'row')
The draws below stay inside these ranges and needn't reach their ends.
All inputs are finite; a program needn't handle non-finite values.
Results may differ from the reference program's by a relative error of at most 0.0057.
Values may be sent and summed in bfloat16 or wider, within the bound.
A program may use at most 128 MiB of HBM per device.

```python
import jax
import jax.numpy as jnp
from jax import lax

M = 3072
C = 128
TICKS = 3
LAYERS = 16


def touch_ends(result, stream_key, least, top_value):
    place = [jax.random.randint(jax.random.fold_in(stream_key, axis), (), 0, length) for axis, length in enumerate(result.shape)]
    widest = result.shape.index(max(result.shape))
    next_to = place[:widest] + [(place[widest] + 1) % result.shape[widest]] + place[widest + 1:]
    return result.at[tuple(place)].set(least).at[tuple(next_to)].set(top_value)


def steps_of(stream_key, shape, shards, low, top_value):
    factor_of = 1.0
    for position, blocks in shards:
        steps = jax.random.uniform(jax.random.fold_in(jax.random.fold_in(stream_key, 6), position), (blocks,), jnp.float32, low / len(shards), top_value / len(shards))
        factor_of = factor_of * jnp.repeat(jnp.exp(steps), shape[position] // blocks).reshape((-1,) + (1,) * (len(shape) - 1 - position))
    return factor_of


def bell_draw(own_key, shape, scale, limit, cuts=(), kind=jnp.bfloat16):
    array = scale * jax.random.normal(own_key, shape, jnp.float32)
    if cuts:
        array = array * steps_of(own_key, shape, cuts, -0.22, 0.18)
    return jnp.clip(array, -limit, limit).astype(kind)


def setup_inputs(seed: int = 0) -> dict:
    key_list = jax.random.split(jax.random.key(seed), 5)
    waves = bell_draw(key_list[0], (LAYERS, M, 4 * C), 1.0, 6.0, ((0, 16), (1, 2)))
    operators = bell_draw(key_list[1], (LAYERS, 4, M, M), (4 * M) ** -0.5, 0.0546875, ((0, 16), (2, 2)))
    sources = bell_draw(key_list[2], (M, 4 * C), 1.0, 6.0, ((0, 2),))
    source_layer = touch_ends(jax.random.randint(key_list[3], (C,), 0, LAYERS), jax.random.fold_in(key_list[3], 1), 0, LAYERS - 1).astype(jnp.int32)
    return dict(waves=waves, operators=operators, sources=sources, source_layer=source_layer)


def combine(real_prod, imag_prod, shot_count):
    real_part = real_prod[:, :shot_count] - imag_prod[:, shot_count:]
    imag_part = real_prod[:, shot_count:] + imag_prod[:, :shot_count]
    return jnp.concatenate([real_part, imag_part], axis=1)


def layer_tick(operator_block, wave_block, layer_id, sources, source_layer):
    full_rows = operator_block.shape[1]
    products = jnp.dot(operator_block.reshape(4 * full_rows, full_rows), wave_block, preferred_element_type=jnp.float32)
    products = products.reshape(4, full_rows, 4 * C)
    half = 2 * C
    down_out = combine(products[0][:, :half], products[1][:, :half], C) + combine(products[2][:, half:], products[3][:, half:], C)
    up_out = combine(products[0][:, half:], products[1][:, half:], C) + combine(products[2][:, :half], products[3][:, :half], C)
    shot_mask = jnp.tile((source_layer == layer_id).astype(jnp.float32), 4)
    source_term = sources.astype(jnp.float32) * shot_mask[None, :]
    down_out = (down_out + source_term[:, :half]).astype(jnp.bfloat16)
    up_out = (up_out + source_term[:, half:]).astype(jnp.bfloat16)
    return down_out, up_out


def reference(waves, operators, sources, source_layer):
    current = waves
    layer_ids = jnp.arange(LAYERS).astype(jnp.int32)
    for sweep_tick in range(TICKS):
        downs, ups = lax.map(lambda packed: layer_tick(packed[0], packed[1], packed[2], sources, source_layer), (operators, current, layer_ids))
        empty_rim = jnp.zeros((1, M, 2 * C), jnp.bfloat16)
        new_down = jnp.concatenate([empty_rim, downs[:-1]], axis=0)
        new_up = jnp.concatenate([ups[1:], empty_rim], axis=0)
        current = jnp.concatenate([new_down, new_up], axis=2)
    return current
```

```python
import functools
import math

import jax
import jax.numpy as jnp
from jax import lax
from jax.experimental import pallas as pl
from jax.experimental.pallas import tpu as pltpu
from jax.sharding import PartitionSpec as P

TICKS = 3
MESH = pl.DeviceIdType.MESH


def swap_halves(first, second):
    half = first.shape[1] // 2
    low = lax.broadcasted_iota(jnp.int32, first.shape, 1) < half
    return (
        jnp.where(low, first, pltpu.roll(second, half, 1)),
        jnp.where(low, pltpu.roll(first, half, 1), second),
    )


def kernel(
    layers, row_parts, chunk,
    waves, operators, sources, source_layer, traces,
    held, current, turned, outgoing, final, source_term,
    load_sem, first_send, send_sem, recv_sem, final_sem,
):
    layer = lax.axis_index("layer")
    part = lax.axis_index("row")
    rows, lanes = outgoing.shape[3], outgoing.shape[4]
    depth = current.shape[3]
    chunks = rows // chunk
    has_above, has_below = layer > 0, layer < layers - 1

    def load(i):
        span = pl.ds(pl.multiple_of(i * chunk, chunk), chunk)
        return pltpu.make_async_copy(operators.at[0, :, span, :], held.at[:, span, :], load_sem.at[i])

    barrier = pltpu.get_barrier_semaphore()
    for d in range(1, row_parts):
        pl.semaphore_signal(barrier, inc=1, device_id=(layer, lax.rem(part + d, row_parts)), device_id_type=MESH)
    for present, other in ((has_above, layer - 1), (has_below, layer + 1)):
        @pl.when(present)
        def _():
            for p in range(row_parts):
                pl.semaphore_signal(barrier, inc=1, device_id=(other, p), device_id_type=MESH)

    def pack(source_of, put):
        @pl.loop(0, chunks)
        def _(i):
            span = pl.ds(pl.multiple_of(i * chunk, chunk), chunk)
            for way in range(2):
                re = source_of(span, 2 * way)
                im = source_of(span, 2 * way + 1)
                for group, packed in enumerate(swap_halves(re, im)):
                    put(i, group, way, packed.astype(jnp.bfloat16))

    def put_wave(i, group, way, packed):
        current[0, group, way, pl.ds(pl.multiple_of(part * rows + i * chunk, chunk), chunk), :] = packed

    pack(lambda span, q: waves[0, span, q * lanes:(q + 1) * lanes].astype(jnp.float32), put_wave)

    peers = row_parts - 1 + row_parts * (has_above.astype(jnp.int32) + has_below.astype(jnp.int32))
    pl.semaphore_wait(barrier, peers)

    own = pl.ds(pl.multiple_of(part * rows, chunk), rows)
    for group in range(2):
        for way in range(2):
            for d in range(1, row_parts):
                pltpu.make_async_remote_copy(
                    src_ref=current.at[0, group, way, own, :],
                    dst_ref=current.at[0, group, way, own, :],
                    send_sem=first_send.at[group, way, d - 1],
                    recv_sem=recv_sem.at[0, group, way, part],
                    device_id=(layer, lax.rem(part + d, row_parts)),
                    device_id_type=MESH,
                ).start()

    for i in range(chunks):
        load(i).start()

    mask = (source_layer[...] == layer).astype(jnp.float32)

    def put_source(i, group, way, packed):
        source_term[group, way, pl.ds(pl.multiple_of(i * chunk, chunk), chunk), :] = packed

    pack(lambda span, q: sources[span, q * lanes:(q + 1) * lanes].astype(jnp.float32) * mask, put_source)

    for way, present in ((0, has_above), (1, has_below)):
        @pl.when(jnp.logical_not(present))
        def _():
            for group in range(2):
                final[group, way] = jnp.zeros((rows, lanes), jnp.bfloat16)
                for tick in range(1, TICKS):
                    @pl.loop(0, depth // chunk)
                    def _(i):
                        span = pl.ds(pl.multiple_of(i * chunk, chunk), chunk)
                        current[tick, group, way, span, :] = jnp.zeros((chunk, lanes), jnp.bfloat16)

    def arrived(tick, group, way, p):
        ref = current.at[tick, group, way, pl.ds(p * rows, rows), :]
        pltpu.make_async_copy(ref, ref, recv_sem.at[tick, group, way, p]).wait()

    @pl.loop(0, 2 * TICKS)
    def _(step):
        tick, group = step // 2, step % 2

        @pl.when(tick == 0)
        def _():
            for p in range(row_parts):
                @pl.when(p != part)
                def _():
                    arrived(tick, group, 0, p)
                    arrived(tick, group, 1, p)

        for way, present in ((0, has_above), (1, has_below)):
            @pl.when(jnp.logical_and(tick > 0, present))
            def _():
                for p in range(row_parts):
                    arrived(tick, group, way, p)

        @pl.loop(0, depth // chunk)
        def _(i):
            span = pl.ds(pl.multiple_of(i * chunk, chunk), chunk)
            low = lax.broadcasted_iota(jnp.int32, (chunk, lanes), 1) < lanes // 2
            for way in range(2):
                rolled = pltpu.roll(current[tick, group, way, span, :].astype(jnp.float32), lanes // 2, 1)
                turned[way, span, :] = jnp.where(low, -rolled, rolled).astype(jnp.bfloat16)

        @pl.loop(0, chunks)
        def _(i):
            span = pl.ds(pl.multiple_of(i * chunk, chunk), chunk)

            @pl.when(step == 0)
            def _():
                load(i).wait()

            down, up = current[tick, group, 0], current[tick, group, 1]
            down_turned, up_turned = turned[0], turned[1]
            total = jnp.dot(held[0, span, :], jnp.concatenate([down, up], 1), preferred_element_type=jnp.float32)
            total += jnp.dot(held[1, span, :], jnp.concatenate([down_turned, up_turned], 1), preferred_element_type=jnp.float32)
            total += jnp.dot(held[2, span, :], jnp.concatenate([up, down], 1), preferred_element_type=jnp.float32)
            total += jnp.dot(held[3, span, :], jnp.concatenate([up_turned, down_turned], 1), preferred_element_type=jnp.float32)
            for way in range(2):
                value = total[:, way * lanes:(way + 1) * lanes] + source_term[group, way, span, :].astype(jnp.float32)
                outgoing[tick, group, way, span, :] = value.astype(jnp.bfloat16)

            there = pl.ds(pl.multiple_of(part * rows + i * chunk, chunk), chunk)
            for way, present, other in ((0, has_below, layer + 1), (1, has_above, layer - 1)):
                @pl.when(jnp.logical_and(present, tick < TICKS - 1))
                def _():
                    for d in range(row_parts - 1, -1, -1):
                        pltpu.make_async_remote_copy(
                            src_ref=outgoing.at[tick, group, way, span, :],
                            dst_ref=current.at[tick + 1, group, way, there, :],
                            send_sem=send_sem.at[tick, group, way, d],
                            recv_sem=recv_sem.at[tick + 1, group, way, part],
                            device_id=(other, lax.rem(part + d, row_parts)),
                            device_id_type=MESH,
                        ).start()

                @pl.when(jnp.logical_and(present, tick == TICKS - 1))
                def _():
                    pltpu.make_async_remote_copy(
                        src_ref=outgoing.at[tick, group, way, span, :],
                        dst_ref=final.at[group, way, span, :],
                        send_sem=send_sem.at[tick, group, way, 0],
                        recv_sem=final_sem.at[group, way],
                        device_id=(other, part),
                        device_id_type=MESH,
                    ).start()

    for way, present in ((0, has_above), (1, has_below)):
        @pl.when(present)
        def _():
            for group in range(2):
                ref = final.at[group, way]
                pltpu.make_async_copy(ref, ref, final_sem.at[group, way]).wait()

    @pl.loop(0, chunks)
    def _(i):
        span = pl.ds(pl.multiple_of(i * chunk, chunk), chunk)
        for way in range(2):
            a = final[0, way, span, :].astype(jnp.float32)
            b = final[1, way, span, :].astype(jnp.float32)
            for q, block in enumerate(swap_halves(a, b)):
                at = (2 * way + q) * lanes
                traces[0, span, at:at + lanes] = block.astype(jnp.bfloat16)

    for group in range(2):
        for way, present in ((0, has_below), (1, has_above)):
            for d in range(1, row_parts):
                ref = current.at[0, group, way, own, :]
                pltpu.make_async_copy(ref, ref, first_send.at[group, way, d - 1]).wait()

            @pl.when(present)
            def _():
                for tick in range(TICKS):
                    for d in range(row_parts if tick < TICKS - 1 else 1):
                        ref = outgoing.at[tick, group, way]
                        pltpu.make_async_copy(ref, ref, send_sem.at[tick, group, way, d]).wait()


def per_device(waves, operators, sources, source_layer):
    layers, row_parts = lax.axis_size("layer"), lax.axis_size("row")
    rows, depth = operators.shape[2], operators.shape[3]
    lanes = waves.shape[2] // 4
    chunk = math.gcd(rows, 256)
    vmem = pl.BlockSpec(memory_space=pltpu.VMEM)
    return pl.pallas_call(
        functools.partial(kernel, layers, row_parts, chunk),
        out_shape=jax.ShapeDtypeStruct(waves.shape, jnp.bfloat16),
        in_specs=[vmem, pl.BlockSpec(memory_space=pl.ANY), vmem, vmem],
        out_specs=vmem,
        scratch_shapes=[
            pltpu.VMEM((4, rows, depth), jnp.bfloat16),
            pltpu.VMEM((TICKS, 2, 2, depth, lanes), jnp.bfloat16),
            pltpu.VMEM((2, depth, lanes), jnp.bfloat16),
            pltpu.VMEM((TICKS, 2, 2, rows, lanes), jnp.bfloat16),
            pltpu.VMEM((2, 2, rows, lanes), jnp.bfloat16),
            pltpu.VMEM((2, 2, rows, lanes), jnp.bfloat16),
            pltpu.SemaphoreType.DMA((rows // chunk,)),
            pltpu.SemaphoreType.DMA((2, 2, max(row_parts - 1, 1))),
            pltpu.SemaphoreType.DMA((TICKS, 2, 2, row_parts)),
            pltpu.SemaphoreType.DMA((TICKS, 2, 2, row_parts)),
            pltpu.SemaphoreType.DMA((2, 2)),
        ],
        compiler_params=pltpu.CompilerParams(
            collective_id=0, has_side_effects=True, vmem_limit_bytes=67043328
        ),
    )(waves, operators, sources, source_layer.reshape(1, lanes))


def solution(mesh):
    return jax.shard_map(
        per_device,
        mesh=mesh,
        in_specs=(P("layer", "row", None), P("layer", None, "row", None), P("row", None), P()),
        out_specs=P("layer", "row", None),
        check_vma=False,
    )
```

```python
import functools
import math

import jax
import jax.numpy as jnp
from jax import lax
from jax.experimental import pallas as pl
from jax.experimental.pallas import tpu as pltpu
from jax.sharding import PartitionSpec as P

TICKS = 3
MESH = pl.DeviceIdType.MESH


def swap_halves(first, second):
    half = first.shape[1] // 2
    low = lax.broadcasted_iota(jnp.int32, first.shape, 1) < half
    return (
        jnp.where(low, first, pltpu.roll(second, half, 1)),
        jnp.where(low, pltpu.roll(first, half, 1), second),
    )


def kernel(
    layers, row_parts, chunk, big,
    waves, operators, sources, source_layer, traces,
    held, current, turned, total, outgoing, final, source_term, stage,
    stage_sem, load_sem, store_sem, first_send, send_sem, recv_sem, final_sem,
):
    layer = lax.axis_index("layer")
    part = lax.axis_index("row")
    rows, lanes = outgoing.shape[3], outgoing.shape[4]
    depth = current.shape[3]
    chunks = rows // chunk
    has_above, has_below = layer > 0, layer < layers - 1

    def piece(i, size=chunk, base=0):
        return pl.ds(pl.multiple_of(base + i * size, chunk), size)

    def load(i):
        span = piece(i, big)
        return pltpu.make_async_copy(operators.at[0, :, span, :], held.at[:, span, :], load_sem.at[i])

    wave_load = pltpu.make_async_copy(waves.at[0], stage, stage_sem.at[0])
    source_load = pltpu.make_async_copy(sources, stage, stage_sem.at[1])
    wave_load.start()

    barrier = pltpu.get_barrier_semaphore()
    for d in range(1, row_parts):
        pl.semaphore_signal(barrier, inc=1, device_id=(layer, lax.rem(part + d, row_parts)), device_id_type=MESH)
    for present, other in ((has_above, layer - 1), (has_below, layer + 1)):
        @pl.when(present)
        def _():
            for p in range(row_parts):
                pl.semaphore_signal(barrier, inc=1, device_id=(other, p), device_id_type=MESH)

    wave_load.wait()
    for i in range(rows // big):
        load(i).start()

    def packed(span):
        for way in range(2):
            at = 2 * way * lanes
            re = stage[span, at:at + lanes].astype(jnp.float32)
            im = stage[span, at + lanes:at + 2 * lanes].astype(jnp.float32)
            yield way, swap_halves(re, im)

    own_base = part * rows

    @pl.loop(0, chunks)
    def _(i):
        for way, groups in packed(piece(i)):
            for group in range(2):
                current[0, group, way, piece(i, chunk, own_base), :] = groups[group].astype(jnp.bfloat16)

    peers = row_parts - 1 + row_parts * (has_above.astype(jnp.int32) + has_below.astype(jnp.int32))
    pl.semaphore_wait(barrier, peers)

    own = piece(0, rows, own_base)
    for group in range(2):
        for way in range(2):
            for d in range(1, row_parts):
                pltpu.make_async_remote_copy(
                    src_ref=current.at[0, group, way, own, :],
                    dst_ref=current.at[0, group, way, own, :],
                    send_sem=first_send.at[group, way, d - 1],
                    recv_sem=recv_sem.at[0, group, way, part],
                    device_id=(layer, lax.rem(part + d, row_parts)),
                    device_id_type=MESH,
                ).start()

    source_load.start()
    source_load.wait()
    mask = (source_layer[...] == layer).astype(jnp.float32)
    pair = jnp.concatenate([mask, mask], 1)
    packed_mask = swap_halves(pair[:, :lanes], pair[:, lanes:])

    @pl.loop(0, chunks)
    def _(i):
        for way, groups in packed(piece(i)):
            for group in range(2):
                source_term[group, way, piece(i), :] = (groups[group] * packed_mask[group]).astype(jnp.bfloat16)

    for way, present in ((0, has_above), (1, has_below)):
        @pl.when(jnp.logical_not(present))
        def _():
            for group in range(2):
                final[group, way] = jnp.zeros((rows, lanes), jnp.bfloat16)
                for tick in range(1, TICKS):
                    @pl.loop(0, depth // chunk)
                    def _(i):
                        current[tick, group, way, piece(i), :] = jnp.zeros((chunk, lanes), jnp.bfloat16)

    def arrived(tick, group, way, p):
        ref = current.at[tick, group, way, piece(0, rows, p * rows), :]
        pltpu.make_async_copy(ref, ref, recv_sem.at[tick, group, way, p]).wait()

    def product(tick, group, span, inner):
        down, up = current[tick, group, 0, inner, :], current[tick, group, 1, inner, :]
        down_turned, up_turned = turned[0], turned[1]
        out = jnp.dot(held[0, span, inner], jnp.concatenate([down, up], 1), preferred_element_type=jnp.float32)
        out += jnp.dot(held[1, span, inner], jnp.concatenate([down_turned, up_turned], 1), preferred_element_type=jnp.float32)
        out += jnp.dot(held[2, span, inner], jnp.concatenate([up, down], 1), preferred_element_type=jnp.float32)
        out += jnp.dot(held[3, span, inner], jnp.concatenate([up_turned, down_turned], 1), preferred_element_type=jnp.float32)
        return out

    @pl.loop(0, 2 * TICKS)
    def _(step):
        tick, group = step // 2, step % 2
        for d in range(row_parts):
            p = lax.rem(part + d, row_parts)
            inner = pl.ds(pl.multiple_of(p * rows, 128), rows)
            if d > 0:
                @pl.when(tick == 0)
                def _():
                    arrived(tick, group, 0, p)
                    arrived(tick, group, 1, p)

            for way, present in ((0, has_above), (1, has_below)):
                @pl.when(jnp.logical_and(tick > 0, present))
                def _():
                    arrived(tick, group, way, p)

            @pl.loop(0, chunks)
            def _(i):
                low = lax.broadcasted_iota(jnp.int32, (chunk, lanes), 1) < lanes // 2
                for way in range(2):
                    block = current[tick, group, way, piece(i, chunk, p * rows), :]
                    rolled = pltpu.roll(block.astype(jnp.float32), lanes // 2, 1)
                    turned[way, piece(i), :] = jnp.where(low, -rolled, rolled).astype(jnp.bfloat16)

            if d < row_parts - 1:
                @pl.loop(0, rows // big)
                def _(i):
                    span = piece(i, big)
                    if d == 0:
                        @pl.when(step == 0)
                        def _():
                            load(i).wait()
                        total[span, :] = product(tick, group, span, inner)
                    else:
                        total[span, :] += product(tick, group, span, inner)
                continue

            @pl.loop(0, chunks)
            def _(i):
                span = piece(i)
                if row_parts == 1:
                    @pl.when(jnp.logical_and(step == 0, i % (big // chunk) == 0))
                    def _():
                        load(i // (big // chunk)).wait()
                out = product(tick, group, span, inner)
                if row_parts > 1:
                    out += total[span, :]
                for way in range(2):
                    value = out[:, way * lanes:(way + 1) * lanes] + source_term[group, way, span, :].astype(jnp.float32)
                    outgoing[tick, group, way, span, :] = value.astype(jnp.bfloat16)

                there = piece(i, chunk, own_base)
                for way, present, other in ((0, has_below, layer + 1), (1, has_above, layer - 1)):
                    @pl.when(jnp.logical_and(present, tick < TICKS - 1))
                    def _():
                        for e in range(row_parts - 1, -1, -1):
                            pltpu.make_async_remote_copy(
                                src_ref=outgoing.at[tick, group, way, span, :],
                                dst_ref=current.at[tick + 1, group, way, there, :],
                                send_sem=send_sem.at[tick, group, way, e],
                                recv_sem=recv_sem.at[tick + 1, group, way, part],
                                device_id=(other, lax.rem(part + e, row_parts)),
                                device_id_type=MESH,
                            ).start()

                    @pl.when(jnp.logical_and(present, tick == TICKS - 1))
                    def _():
                        pltpu.make_async_remote_copy(
                            src_ref=outgoing.at[tick, group, way, span, :],
                            dst_ref=final.at[group, way, span, :],
                            send_sem=send_sem.at[tick, group, way, 0],
                            recv_sem=final_sem.at[group, way, i],
                            device_id=(other, part),
                            device_id_type=MESH,
                        ).start()

    def store(i):
        return pltpu.make_async_copy(stage.at[piece(i), :], traces.at[0, piece(i), :], store_sem.at[i])

    @pl.loop(0, chunks)
    def _(i):
        span = piece(i)
        for way, present in ((0, has_above), (1, has_below)):
            @pl.when(present)
            def _():
                for group in range(2):
                    ref = final.at[group, way, span, :]
                    pltpu.make_async_copy(ref, ref, final_sem.at[group, way, i]).wait()
            a = final[0, way, span, :].astype(jnp.float32)
            b = final[1, way, span, :].astype(jnp.float32)
            for q, block in enumerate(swap_halves(a, b)):
                at = (2 * way + q) * lanes
                stage[span, at:at + lanes] = block.astype(jnp.bfloat16)
        store(i).start()

    for group in range(2):
        for way, present in ((0, has_below), (1, has_above)):
            for d in range(1, row_parts):
                ref = current.at[0, group, way, own, :]
                pltpu.make_async_copy(ref, ref, first_send.at[group, way, d - 1]).wait()

            @pl.when(present)
            def _():
                for tick in range(TICKS):
                    for d in range(row_parts if tick < TICKS - 1 else 1):
                        ref = outgoing.at[tick, group, way]
                        pltpu.make_async_copy(ref, ref, send_sem.at[tick, group, way, d]).wait()

    for i in range(chunks):
        store(i).wait()


def per_device(waves, operators, sources, source_layer):
    layers, row_parts = lax.axis_size("layer"), lax.axis_size("row")
    rows, depth = operators.shape[2], operators.shape[3]
    lanes = waves.shape[2] // 4
    chunk, big = math.gcd(rows, 256), math.gcd(rows, 512)
    anywhere = pl.BlockSpec(memory_space=pl.ANY)
    traces = pl.pallas_call(
        functools.partial(kernel, layers, row_parts, chunk, big),
        out_shape=jax.ShapeDtypeStruct(waves.shape, jnp.bfloat16),
        in_specs=[anywhere, anywhere, anywhere, pl.BlockSpec(memory_space=pltpu.VMEM)],
        out_specs=anywhere,
        scratch_shapes=[
            pltpu.VMEM((4, rows, depth), jnp.bfloat16),
            pltpu.VMEM((TICKS, 2, 2, depth, lanes), jnp.bfloat16),
            pltpu.VMEM((2, rows, lanes), jnp.bfloat16),
            pltpu.VMEM((rows, 2 * lanes), jnp.float32),
            pltpu.VMEM((TICKS, 2, 2, rows, lanes), jnp.bfloat16),
            pltpu.VMEM((2, 2, rows, lanes), jnp.bfloat16),
            pltpu.VMEM((2, 2, rows, lanes), jnp.bfloat16),
            pltpu.VMEM((rows, 4 * lanes), jnp.bfloat16),
            pltpu.SemaphoreType.DMA((2,)),
            pltpu.SemaphoreType.DMA((rows // big,)),
            pltpu.SemaphoreType.DMA((rows // chunk,)),
            pltpu.SemaphoreType.DMA((2, 2, max(row_parts - 1, 1))),
            pltpu.SemaphoreType.DMA((TICKS, 2, 2, row_parts)),
            pltpu.SemaphoreType.DMA((TICKS, 2, 2, row_parts)),
            pltpu.SemaphoreType.DMA((2, 2, rows // chunk)),
        ],
        compiler_params=pltpu.CompilerParams(
            collective_id=0, has_side_effects=True, vmem_limit_bytes=67043328
        ),
    )(waves, operators, sources, source_layer.reshape(1, lanes))
    layer = lax.axis_index("layer")
    upgoing = lax.broadcasted_iota(jnp.int32, waves.shape, 2) >= 2 * lanes
    edge = jnp.where(upgoing, layer == layers - 1, layer == 0)
    return jnp.where(edge, jnp.zeros_like(traces), traces)


def solution(mesh):
    return jax.shard_map(
        per_device,
        mesh=mesh,
        in_specs=(P("layer", "row", None), P("layer", None, "row", None), P("row", None), P()),
        out_specs=P("layer", "row", None),
        check_vma=False,
    )
```

```python
import functools
import math

import jax
import jax.numpy as jnp
from jax import lax
from jax.experimental import pallas as pl
from jax.experimental.pallas import tpu as pltpu
from jax.sharding import PartitionSpec as P

TICKS = 3
RELAY = 4
MESH = pl.DeviceIdType.MESH


def swap_halves(first, second):
    half = first.shape[1] // 2
    low = lax.broadcasted_iota(jnp.int32, first.shape, 1) < half
    return (
        jnp.where(low, first, pltpu.roll(second, half, 1)),
        jnp.where(low, pltpu.roll(first, half, 1), second),
    )


def kernel(
    layers, row_parts, chunk, big,
    waves, operators, sources, source_layer, traces,
    held, current, turned, total, outgoing, final, source_term, stage,
    stage_sem, load_sem, store_sem, row_send, send_sem, recv_sem, final_sem,
):
    layer = lax.axis_index("layer")
    part = lax.axis_index("row")
    rows, lanes = outgoing.shape[3], outgoing.shape[4]
    depth = current.shape[3]
    chunks = rows // chunk
    has_above, has_below = layer > 0, layer < layers - 1

    def piece(i, size=chunk, base=0):
        return pl.ds(pl.multiple_of(base + i * size, chunk), size)

    def load(i):
        span = piece(i, big)
        return pltpu.make_async_copy(operators.at[0, :, span, :], held.at[:, span, :], load_sem.at[i])

    wave_load = pltpu.make_async_copy(waves.at[0], stage, stage_sem.at[0])
    source_load = pltpu.make_async_copy(sources, stage, stage_sem.at[1])
    wave_load.start()

    barrier = pltpu.get_barrier_semaphore()
    for d in range(1, row_parts):
        pl.semaphore_signal(barrier, inc=1, device_id=(layer, lax.rem(part + d, row_parts)), device_id_type=MESH)
    for present, other in ((has_above, layer - 1), (has_below, layer + 1)):
        @pl.when(present)
        def _():
            pl.semaphore_signal(barrier, inc=1, device_id=(other, part), device_id_type=MESH)

    wave_load.wait()
    for i in range(rows // big):
        load(i).start()

    def packed(span):
        for way in range(2):
            at = 2 * way * lanes
            re = stage[span, at:at + lanes].astype(jnp.float32)
            im = stage[span, at + lanes:at + 2 * lanes].astype(jnp.float32)
            yield way, swap_halves(re, im)

    own_base = part * rows

    peers = row_parts - 1 + has_above.astype(jnp.int32) + has_below.astype(jnp.int32)
    pl.semaphore_wait(barrier, peers)

    def forward(tick, group, way, span):
        for d in range(1, row_parts):
            pltpu.make_async_remote_copy(
                src_ref=current.at[tick, group, way, span, :],
                dst_ref=current.at[tick, group, way, span, :],
                send_sem=row_send.at[tick, group, way, d - 1],
                recv_sem=recv_sem.at[tick, group, way, part],
                device_id=(layer, lax.rem(part + d, row_parts)),
                device_id_type=MESH,
            ).start()

    @pl.loop(0, chunks)
    def _(i):
        span = piece(i, chunk, own_base)
        for way, groups in packed(piece(i)):
            for group in range(2):
                current[0, group, way, span, :] = groups[group].astype(jnp.bfloat16)
        forward(0, 0, 0, span)
        forward(0, 0, 1, span)

    own = piece(0, rows, own_base)
    forward(0, 1, 0, own)
    forward(0, 1, 1, own)

    source_load.start()
    source_load.wait()
    mask = (source_layer[...] == layer).astype(jnp.float32)
    pair = jnp.concatenate([mask, mask], 1)
    packed_mask = swap_halves(pair[:, :lanes], pair[:, lanes:])

    @pl.loop(0, chunks)
    def _(i):
        for way, groups in packed(piece(i)):
            for group in range(2):
                source_term[group, way, piece(i), :] = (groups[group] * packed_mask[group]).astype(jnp.bfloat16)

    for way, present in ((0, has_above), (1, has_below)):
        @pl.when(jnp.logical_not(present))
        def _():
            for group in range(2):
                final[group, way] = jnp.zeros((rows, lanes), jnp.bfloat16)
                for tick in range(1, TICKS):
                    @pl.loop(0, depth // chunk)
                    def _(i):
                        current[tick, group, way, piece(i), :] = jnp.zeros((chunk, lanes), jnp.bfloat16)

    def arrived(tick, group, way, p):
        ref = current.at[tick, group, way, piece(0, rows, p * rows), :]
        pltpu.make_async_copy(ref, ref, recv_sem.at[tick, group, way, p]).wait()

    def product(tick, group, span, inner):
        down, up = current[tick, group, 0, inner, :], current[tick, group, 1, inner, :]
        down_turned, up_turned = turned[0], turned[1]
        out = jnp.dot(held[0, span, inner], jnp.concatenate([down, up], 1), preferred_element_type=jnp.float32)
        out += jnp.dot(held[1, span, inner], jnp.concatenate([down_turned, up_turned], 1), preferred_element_type=jnp.float32)
        out += jnp.dot(held[2, span, inner], jnp.concatenate([up, down], 1), preferred_element_type=jnp.float32)
        out += jnp.dot(held[3, span, inner], jnp.concatenate([up_turned, down_turned], 1), preferred_element_type=jnp.float32)
        return out

    def take_next(step):
        tick, group = step // 2, step % 2
        for way, present in ((0, has_above), (1, has_below)):
            @pl.when(jnp.logical_and(present, jnp.logical_and(step >= 2, step < 2 * TICKS)))
            def _():
                arrived(tick, group, way, part)
                forward(tick, group, way, own)

    @pl.loop(0, 2 * TICKS)
    def _(step):
        tick, group = step // 2, step % 2
        for d in range(row_parts):
            p = lax.rem(part + d, row_parts)
            inner = pl.ds(pl.multiple_of(p * rows, 128), rows)
            if d == min(1, row_parts - 1):
                take_next(step + 1)

            if d > 0:
                @pl.when(tick == 0)
                def _():
                    arrived(tick, group, 0, p)
                    arrived(tick, group, 1, p)

                for way, present in ((0, has_above), (1, has_below)):
                    @pl.when(jnp.logical_and(tick > 0, present))
                    def _():
                        arrived(tick, group, way, p)

            @pl.loop(0, chunks)
            def _(i):
                low = lax.broadcasted_iota(jnp.int32, (chunk, lanes), 1) < lanes // 2
                for way in range(2):
                    block = current[tick, group, way, piece(i, chunk, p * rows), :]
                    rolled = pltpu.roll(block.astype(jnp.float32), lanes // 2, 1)
                    turned[way, piece(i), :] = jnp.where(low, -rolled, rolled).astype(jnp.bfloat16)

            if d < row_parts - 1:
                @pl.loop(0, rows // big)
                def _(i):
                    span = piece(i, big)
                    if d == 0:
                        @pl.when(step == 0)
                        def _():
                            load(i).wait()
                        total[span, :] = product(tick, group, span, inner)
                    else:
                        total[span, :] += product(tick, group, span, inner)
                continue

            @pl.loop(0, chunks)
            def _(i):
                span = piece(i)
                if row_parts == 1:
                    @pl.when(jnp.logical_and(step == 0, i % (big // chunk) == 0))
                    def _():
                        load(i // (big // chunk)).wait()
                out = product(tick, group, span, inner)
                if row_parts > 1:
                    out += total[span, :]
                for way in range(2):
                    value = out[:, way * lanes:(way + 1) * lanes] + source_term[group, way, span, :].astype(jnp.float32)
                    outgoing[tick, group, way, span, :] = value.astype(jnp.bfloat16)

                there = piece(i, chunk, own_base)
                for way, present, other in ((0, has_below, layer + 1), (1, has_above, layer - 1)):
                    @pl.when(jnp.logical_and(present, tick < TICKS - 1))
                    def _():
                        pltpu.make_async_remote_copy(
                            src_ref=outgoing.at[tick, group, way, span, :],
                            dst_ref=current.at[tick + 1, group, way, there, :],
                            send_sem=send_sem.at[tick, group, way],
                            recv_sem=recv_sem.at[tick + 1, group, way, part],
                            device_id=(other, part),
                            device_id_type=MESH,
                        ).start()

                    @pl.when(jnp.logical_and(present, tick == TICKS - 1))
                    def _():
                        pltpu.make_async_remote_copy(
                            src_ref=outgoing.at[tick, group, way, span, :],
                            dst_ref=final.at[group, way, span, :],
                            send_sem=send_sem.at[tick, group, way],
                            recv_sem=final_sem.at[group, way, i],
                            device_id=(other, part),
                            device_id_type=MESH,
                        ).start()

    def store(i):
        return pltpu.make_async_copy(stage.at[piece(i), :], traces.at[0, piece(i), :], store_sem.at[i])

    @pl.loop(0, chunks)
    def _(i):
        span = piece(i)
        for way, present in ((0, has_above), (1, has_below)):
            @pl.when(present)
            def _():
                for group in range(2):
                    ref = final.at[group, way, span, :]
                    pltpu.make_async_copy(ref, ref, final_sem.at[group, way, i]).wait()
            a = final[0, way, span, :].astype(jnp.float32)
            b = final[1, way, span, :].astype(jnp.float32)
            for q, block in enumerate(swap_halves(a, b)):
                at = (2 * way + q) * lanes
                stage[span, at:at + lanes] = block.astype(jnp.bfloat16)
        store(i).start()

    def sent(tick, group, way):
        for d in range(1, row_parts):
            ref = current.at[tick, group, way, own, :]
            pltpu.make_async_copy(ref, ref, row_send.at[tick, group, way, d - 1]).wait()

    for group in range(2):
        for way, came, goes in ((0, has_above, has_below), (1, has_below, has_above)):
            sent(0, group, way)

            @pl.when(came)
            def _():
                for tick in range(1, TICKS):
                    sent(tick, group, way)

            @pl.when(goes)
            def _():
                for tick in range(TICKS):
                    ref = outgoing.at[tick, group, way]
                    pltpu.make_async_copy(ref, ref, send_sem.at[tick, group, way]).wait()

    for i in range(chunks):
        store(i).wait()


def relay(traces, result, buffer, in_sem, out_sem):
    size = traces.shape[1] // RELAY
    spans = [pl.ds(i * size, size) for i in range(RELAY)]
    takes = [pltpu.make_async_copy(traces.at[:, s], buffer.at[:, s], in_sem.at[i]) for i, s in enumerate(spans)]
    puts = [pltpu.make_async_copy(buffer.at[:, s], result.at[:, s], out_sem.at[i]) for i, s in enumerate(spans)]
    for take in takes:
        take.start()
    for take, put in zip(takes, puts):
        take.wait()
        put.start()
    for put in puts:
        put.wait()


def per_device(waves, operators, sources, source_layer):
    layers, row_parts = lax.axis_size("layer"), lax.axis_size("row")
    rows, depth = operators.shape[2], operators.shape[3]
    lanes = waves.shape[2] // 4
    chunk, big = math.gcd(rows, 256), math.gcd(rows, 512)
    anywhere = pl.BlockSpec(memory_space=pl.ANY)
    traces = pl.pallas_call(
        functools.partial(kernel, layers, row_parts, chunk, big),
        out_shape=jax.ShapeDtypeStruct(waves.shape, jnp.bfloat16),
        in_specs=[anywhere, anywhere, anywhere, pl.BlockSpec(memory_space=pltpu.VMEM)],
        out_specs=anywhere,
        scratch_shapes=[
            pltpu.VMEM((4, rows, depth), jnp.bfloat16),
            pltpu.VMEM((TICKS, 2, 2, depth, lanes), jnp.bfloat16),
            pltpu.VMEM((2, rows, lanes), jnp.bfloat16),
            pltpu.VMEM((rows, 2 * lanes), jnp.float32),
            pltpu.VMEM((TICKS, 2, 2, rows, lanes), jnp.bfloat16),
            pltpu.VMEM((2, 2, rows, lanes), jnp.bfloat16),
            pltpu.VMEM((2, 2, rows, lanes), jnp.bfloat16),
            pltpu.VMEM((rows, 4 * lanes), jnp.bfloat16),
            pltpu.SemaphoreType.DMA((2,)),
            pltpu.SemaphoreType.DMA((rows // big,)),
            pltpu.SemaphoreType.DMA((rows // chunk,)),
            pltpu.SemaphoreType.DMA((TICKS, 2, 2, max(row_parts - 1, 1))),
            pltpu.SemaphoreType.DMA((TICKS, 2, 2)),
            pltpu.SemaphoreType.DMA((TICKS, 2, 2, row_parts)),
            pltpu.SemaphoreType.DMA((2, 2, rows // chunk)),
        ],
        compiler_params=pltpu.CompilerParams(
            collective_id=0, has_side_effects=True, vmem_limit_bytes=67043328
        ),
    )(waves, operators, sources, source_layer.reshape(1, lanes))
    return pl.pallas_call(
        relay,
        out_shape=jax.ShapeDtypeStruct(traces.shape, traces.dtype),
        in_specs=[anywhere],
        out_specs=anywhere,
        scratch_shapes=[
            pltpu.VMEM(traces.shape, traces.dtype),
            pltpu.SemaphoreType.DMA((RELAY,)),
            pltpu.SemaphoreType.DMA((RELAY,)),
        ],
    )(traces)


def solution(mesh):
    return jax.shard_map(
        per_device,
        mesh=mesh,
        in_specs=(P("layer", "row", None), P("layer", None, "row", None), P("row", None), P()),
        out_specs=P("layer", "row", None),
        check_vma=False,
    )
```
